512 devices in a mesh: site: 128 (over z, x_hi, y), src: 4 (over x_lo, core).
Axes of the slice: x: 4 (x_hi: 2, x_lo: 2; x = x_hi * 2 + x_lo), y: 8, z: 8, core: 2. Of those that a mesh axis runs over, the one named last changes fastest.
Arguments:
- source: float32 [2, 12, 4, 12, 32768], P(None, None, 'src', None, 'site'), may hold values from -6 to 6
- basis: bfloat16 [2, 12, 128, 32768], P(None, None, None, 'site'), may hold values from -0.078125 to 0.078125
- compressed: bfloat16 [2, 512, 128, 12, 128], P(None, 'src', 'site'), may hold values from -0.0390625 to 0.0390625
- eigenvalues: float32 [512], P('src'), may hold values from 0.01 to 0.1
- links: float32 [2, 4, 3, 3, 32768], P(None, None, None, None, 'site'), may hold values from -2.5 to 2.5
Outputs:
- residual: float32 [2, 12, 4, 12, 32768], P(None, None, 'src', None, 'site')
The draws below stay inside these ranges and needn't reach their ends.
All inputs are finite; a program needn't handle non-finite values.
Results may differ from the reference program's by a relative error of at most 0.0095.
Values may be sent and summed in bfloat16 or wider, within the bound.
A program may use at most 64 MiB of HBM per device.

```python
import math
import jax
import jax.numpy as jnp
from jax import lax

EDGE = 4
LS = 12
NV = 128
K = 512
SOURCES = 4
BLOCKS = 128
SITES = 32768


def raised(result, own_key, source, target, shards_of, factor):
    owner, partner = [(jnp.arange(result.shape[axis_at]) // (result.shape[axis_at] // shards_of)).reshape([-1 if axis == axis_at else 1 for axis in range(result.ndim)]) for axis_at in (source, target)]
    chosen = jax.random.permutation(own_key, shards_of)[partner]
    strong = (owner == chosen) | (owner == (partner + shards_of // 2) % shards_of)
    return jnp.where(strong, factor * result, result)


def block_scale(key, shape, pieces, smallest, high):
    def one(dim, shards_of):
        steps = jax.random.uniform(jax.random.fold_in(jax.random.fold_in(key, 6), dim), (shards_of,), jnp.float32, smallest / len(pieces), high / len(pieces))
        return jnp.repeat(jnp.exp(steps), shape[dim] // shards_of).reshape((-1,) + (1,) * (len(shape) - dim - 1))

    factor_of = one(*pieces[0])
    for cut in pieces[1:]:
        factor_of = factor_of * one(*cut)
    return factor_of


def noise(own_key, extent, spread, limit, shards=(), dtype=jnp.bfloat16):
    values = spread * jax.random.normal(own_key, extent, jnp.float32)
    if shards:
        values = values * block_scale(own_key, extent, shards, -0.22, 0.18)
    return jnp.clip(values, -limit, limit).astype(dtype)


def noise_with(own_key, dims, deviation, reach, pieces, heavy, kind=jnp.bfloat16):
    result = deviation * jax.random.normal(own_key, dims, jnp.float32)
    if pieces:
        result = result * block_scale(own_key, dims, pieces, -0.22, 0.18)
    return jnp.clip(raised(result, jax.random.fold_in(own_key, 3), *heavy), -reach, reach).astype(kind)


def setup_inputs(seed: int = 0) -> dict:
    seeds = jax.random.split(jax.random.key(seed), 6)
    source = noise(seeds[0], (2, 12, SOURCES, LS, SITES), 1.0, 6.0, ((2, 4), (4, 128)), jnp.float32)
    basis = noise(seeds[1], (2, 12, NV, SITES), (24 * EDGE ** 4) ** -0.5, 0.078125, ((3, 128),))
    compressed = noise_with(seeds[2], (2, K, BLOCKS, LS, NV), (2 * BLOCKS * LS * NV) ** -0.5, 0.0390625, ((1, 4), (2, 128)), (2, 1, 128, 5.5))
    eigenvalues = jnp.clip(jnp.exp(math.log(0.1) - 2.3025851 * jax.random.uniform(seeds[3], (K,), jnp.float32) ** block_scale(seeds[3], (K,), ((0, 4),), -0.2, 0.2)), 0.01, 0.1)
    links = noise(seeds[4], (2, 4, 3, 3, SITES), 6 ** -0.5, 2.5, ((4, 128),), jnp.float32)
    return dict(source=source, basis=basis, compressed=compressed, eigenvalues=eigenvalues, links=links)


FIFTH_MASS = 0.4
WALL_HEIGHT = 1.8


def times_i(values):
    return jnp.stack([-values[1], values[0]])


def times_minus_i(values):
    return jnp.stack([values[1], -values[0]])


def spin_e(direction, lower_spins):
    first_spin = lower_spins[:, :, :, 0]
    second_spin = lower_spins[:, :, :, 1]
    if direction == 0:
        spin_pair = (times_i(second_spin), times_i(first_spin))
    elif direction == 1:
        spin_pair = (second_spin, -first_spin)
    elif direction == 2:
        spin_pair = (times_i(first_spin), -times_i(second_spin))
    else:
        spin_pair = (first_spin, second_spin)
    return jnp.stack(spin_pair, axis=3)


def spin_e_dagger(direction, upper_spins):
    first_spin = upper_spins[:, :, :, 0]
    second_spin = upper_spins[:, :, :, 1]
    if direction == 0:
        spin_pair = (times_minus_i(second_spin), times_minus_i(first_spin))
    elif direction == 1:
        spin_pair = (-second_spin, first_spin)
    elif direction == 2:
        spin_pair = (times_minus_i(first_spin), times_i(second_spin))
    else:
        spin_pair = (first_spin, second_spin)
    return jnp.stack(spin_pair, axis=3)


def colour_times(link_mat, spinor):
    real_terms = []
    imaginary_terms = []
    for colour in range(3):
        link_real = link_mat[0, :, colour]
        link_imag = link_mat[1, :, colour]
        spin_real = spinor[0, ..., colour:colour + 1, :]
        spin_imag = spinor[1, ..., colour:colour + 1, :]
        real_terms.append(link_real * spin_real - link_imag * spin_imag)
        imaginary_terms.append(link_real * spin_imag + link_imag * spin_real)
    return jnp.stack([real_terms[0] + real_terms[1] + real_terms[2], imaginary_terms[0] + imaginary_terms[1] + imaginary_terms[2]])


def colour_dagger(link_mat, spinor):
    real_terms = []
    imaginary_terms = []
    for colour in range(3):
        link_real = link_mat[0, colour]
        link_imag = link_mat[1, colour]
        spin_real = spinor[0, ..., colour:colour + 1, :]
        spin_imag = spinor[1, ..., colour:colour + 1, :]
        real_terms.append(link_real * spin_real + link_imag * spin_imag)
        imaginary_terms.append(link_real * spin_imag - link_imag * spin_real)
    return jnp.stack([real_terms[0] + real_terms[1] + real_terms[2], imaginary_terms[0] + imaginary_terms[1] + imaginary_terms[2]])


def roll_site(spinor, direction, total_amount):
    lead_shape = spinor.shape[:-1]
    volume = spinor.shape[-1]
    lead_count = len(lead_shape)
    time_blocks = volume // (8 * EDGE ** 4)
    shaped = spinor.reshape(lead_shape + (time_blocks, 2, 2, 2, EDGE, EDGE, EDGE, EDGE))
    lead_perm = tuple(range(lead_count))
    forward = tuple(lead_count + shift_offset for shift_offset in (0, 4, 1, 5, 2, 6, 3, 7))
    lattice = jnp.transpose(shaped, lead_perm + forward)
    lattice = lattice.reshape(lead_shape + (time_blocks * EDGE, 2 * EDGE, 2 * EDGE, 2 * EDGE))
    rolled = jnp.roll(lattice, total_amount, axis=lead_count + 3 - direction)
    rolled = rolled.reshape(lead_shape + (time_blocks, EDGE, 2, EDGE, 2, EDGE, 2, EDGE))
    backward = tuple(lead_count + shift_offset for shift_offset in (0, 2, 4, 6, 1, 3, 5, 7))
    return jnp.transpose(rolled, lead_perm + backward).reshape(lead_shape + (volume,))


def both_hops(direction, ahead_half, behind_half, link_mat):
    moved = colour_times(link_mat, ahead_half)
    ahead_full = jnp.concatenate([moved, -spin_e_dagger(direction, moved)], axis=3)
    behind_full = jnp.concatenate([behind_half, spin_e_dagger(direction, behind_half)], axis=3)
    return ahead_full + behind_full


def hop_direction(guess, link_mat, direction):
    upper_spins = guess[:, :, :, 0:2]
    projected = spin_e(direction, guess[:, :, :, 2:4])
    ahead_half = roll_site(upper_spins - projected, direction, -1)
    behind_half = roll_site(colour_dagger(link_mat, upper_spins + projected), direction, 1)
    return both_hops(direction, ahead_half, behind_half, link_mat)


def fifth_terms(guess):
    ahead = jnp.concatenate([guess[:, :, 1:], -FIFTH_MASS * guess[:, :, :1]], axis=2)
    behind = jnp.concatenate([-FIFTH_MASS * guess[:, :, -1:], guess[:, :, :-1]], axis=2)
    return jnp.concatenate([behind[:, :, :, 0:2], ahead[:, :, :, 2:4]], axis=3)


def apply_operator(guess, links):
    hopping = hop_direction(guess, links[:, 0], 0)
    for direction in range(1, 4):
        hopping = hopping + hop_direction(guess, links[:, direction], direction)
    return (5.0 - WALL_HEIGHT) * guess - 0.5 * hopping - fifth_terms(guess)


def dot_last(left_rows, right_rows):
    return lax.dot_general(left_rows, right_rows, (((1,), (1,)), ((), ())), preferred_element_type=jnp.float32)


def dot_plain(left_rows, right_rows):
    return jnp.dot(left_rows, right_rows, preferred_element_type=jnp.float32)


def project_block(operands):
    block_source, block_basis = operands
    proj_real = dot_last(block_source[0], block_basis[0]) + dot_last(block_source[1], block_basis[1])
    proj_imag = dot_last(block_source[1], block_basis[0]) - dot_last(block_source[0], block_basis[1])
    return jnp.stack([proj_real, proj_imag])


def prolong_block(operands):
    block_coarse, block_basis = operands
    guess_real = dot_plain(block_coarse[0], block_basis[0]) - dot_plain(block_coarse[1], block_basis[1])
    guess_imag = dot_plain(block_coarse[0], block_basis[1]) + dot_plain(block_coarse[1], block_basis[0])
    return jnp.stack([guess_real, guess_imag])


def reference(source, basis, compressed, eigenvalues, links):
    spin_source = jnp.transpose(source, (0, 2, 3, 1, 4))
    vector_basis = jnp.transpose(basis, (0, 2, 1, 3))
    sources = spin_source.shape[1]
    sites = spin_source.shape[4]
    volume = EDGE ** 4
    blocks = sites // volume
    row_count = sources * LS
    low_source = spin_source.astype(jnp.bfloat16).reshape(2, row_count, 12, blocks, volume)
    source_blocks = jnp.transpose(low_source, (3, 0, 1, 2, 4)).reshape(blocks, 2, row_count, 12 * volume)
    basis_blocks = jnp.transpose(vector_basis.reshape(2, NV, 12, blocks, volume), (3, 0, 1, 2, 4)).reshape(blocks, 2, NV, 12 * volume)
    projections = lax.map(project_block, (source_blocks, basis_blocks))
    low_proj = projections.astype(jnp.bfloat16).reshape(blocks, 2, sources, LS, NV)
    low_proj = jnp.transpose(low_proj, (1, 2, 0, 3, 4)).reshape(2, sources, blocks * LS * NV)
    coarse_table = compressed.reshape(2, compressed.shape[1], blocks * LS * NV)
    amp_real = dot_last(low_proj[0], coarse_table[0]) + dot_last(low_proj[1], coarse_table[1])
    amp_imag = dot_last(low_proj[1], coarse_table[0]) - dot_last(low_proj[0], coarse_table[1])
    weights = (jnp.stack([amp_real, amp_imag]) / eigenvalues).astype(jnp.bfloat16)
    coarse_real = dot_plain(weights[0], coarse_table[0]) - dot_plain(weights[1], coarse_table[1])
    coarse_imag = dot_plain(weights[0], coarse_table[1]) + dot_plain(weights[1], coarse_table[0])
    low_coarse = jnp.stack([coarse_real, coarse_imag]).astype(jnp.bfloat16).reshape(2, sources, blocks, LS, NV)
    coarse_blocks = jnp.transpose(low_coarse, (2, 0, 1, 3, 4)).reshape(blocks, 2, row_count, NV)
    guess_blocks = lax.map(prolong_block, (coarse_blocks, basis_blocks))
    guess = jnp.transpose(guess_blocks.reshape(blocks, 2, sources, LS, 12, volume), (1, 2, 3, 4, 0, 5))
    guess = guess.reshape(2, sources, LS, 4, 3, sites)
    by_source = jnp.moveaxis(guess, 1, 0)[:, :, None]

    def apply_single(single_source):
        return apply_operator(single_source, links)

    applied = lax.map(apply_single, by_source)
    applied = jnp.moveaxis(applied[:, :, 0], 0, 1).reshape(spin_source.shape)
    return jnp.transpose(spin_source - applied, (0, 3, 1, 2, 4))
```

```python
import functools

import jax
import jax.numpy as jnp
from jax import lax
from jax.experimental import pallas as pl
from jax.experimental.pallas import tpu as pltpu
from jax.sharding import PartitionSpec as P

MESH = pl.DeviceIdType.MESH
F32 = jnp.float32
BF16 = jnp.bfloat16

EDGE = 4
LS = 12
NV = 128
VOL = EDGE**4
NS = 4
FIFTH_MASS = 0.4
WALL_HEIGHT = 1.8
VMEM_LIMIT = 48 * 1024 * 1024


def dot_nt(left, right):
    return lax.dot_general(left, right, (((1,), (1,)), ((), ())), preferred_element_type=F32)


def dot_nn(left, right):
    return jnp.dot(left, right, preferred_element_type=F32)


def site_selector(direction, level):
    stride = EDGE**direction
    lane = lax.broadcasted_iota(jnp.int32, (VOL, 128), 0)
    col = lax.broadcasted_iota(jnp.int32, (VOL, 128), 1)
    cell = col & 63
    site = (cell & (stride - 1)) + level * stride + (cell // stride) * (stride * EDGE)
    match = lane == site
    low = jnp.where(match & (col < 64), 1.0, 0.0).astype(BF16)
    high = jnp.where(match & (col >= 64), 1.0, 0.0).astype(BF16)
    return low, high


def times_i(value):
    return (-value[1], value[0])


def neg(value):
    return (-value[0], -value[1])


def add(left, right):
    return (left[0] + right[0], left[1] + right[1])


def sub(left, right):
    return (left[0] - right[0], left[1] - right[1])


def spin_e(direction, first, second):
    if direction == 0:
        return times_i(second), times_i(first)
    if direction == 1:
        return second, neg(first)
    if direction == 2:
        return times_i(first), neg(times_i(second))
    return first, second


def spin_e_dagger(direction, first, second):
    if direction == 0:
        return neg(times_i(second)), neg(times_i(first))
    if direction == 1:
        return neg(second), first
    if direction == 2:
        return neg(times_i(first)), times_i(second)
    return first, second


def half_spinors(direction, load):
    minus = [None] * 6
    plus = [None] * 6
    for colour in range(3):
        lowers = spin_e(direction, load(6 + colour), load(9 + colour))
        for spin in range(2):
            upper = load(3 * spin + colour)
            minus[3 * spin + colour] = sub(upper, lowers[spin])
            plus[3 * spin + colour] = add(upper, lowers[spin])
    return minus, plus


def neighbours(block, blocks):
    ahead = []
    behind = []
    for direction in range(3):
        step = 1 << direction
        other = block + step - 2 * step * ((block // step) % 2)
        ahead.append(other)
        behind.append(other)
    ahead.append((block + 8) % blocks)
    behind.append((block + blocks - 8) % blocks)
    return ahead, behind


def guess_kernel(
    blocks,
    src_ref, basis_ref, comp_ref, eig_ref, links_ref,
    guess_out, fwd_out, bwd_out, rlinks_out,
    low_src, gathered, trans, parts, incoming, sums_t, sums_y,
    link_rows, link_in, fwd_send, bwd_send, fwd_in, bwd_in,
    gather_s, gather_r, parts_s, parts_r, t_s, t_r, y_s, y_r,
    link_s, link_r, fwd_s, fwd_r, bwd_s, bwd_r,
):
    block = lax.axis_index("site")
    mine = lax.axis_index("src")
    slices = blocks // 8
    time = block // 8
    place = block % 8
    ahead, behind = neighbours(block, blocks)

    def src_peer(step):
        return (block, (mine + step) % NS)

    def time_peer(step):
        return (((time + step) % slices) * 8 + place, mine)

    def place_peer(step):
        return (time * 8 + (place + step) % 8, mine)

    barrier = pltpu.get_barrier_semaphore()
    for count, peer in ((NS, src_peer), (slices, time_peer), (8, place_peer)):
        for step in range(1, count):
            pl.semaphore_signal(barrier, inc=1, device_id=peer(step), device_id_type=MESH)

    for a in range(12):
        for part in range(2):
            for half in range(2):
                rows = src_ref[pl.ds(24 * (part * 12 + a) + half, LS, stride=2), :]
                low_src[a, part * 16 : part * 16 + LS, half * 128 : half * 128 + 128] = rows
    product = jnp.zeros((32, 256), F32)
    for a in range(12):
        tile = basis_ref[:, a].reshape(2 * NV, VOL)
        product += dot_nt(low_src[a].astype(BF16), tile)
    gathered[0, 0] = (product[0:16, 0:128] + product[16:32, 128:256]).astype(BF16)
    gathered[0, 1] = (product[16:32, 0:128] - product[0:16, 128:256]).astype(BF16)

    for direction in range(4):
        for part in range(2):
            for row in range(3):
                for colour in range(3):
                    at = part * 9 + row * 3 + colour
                    link_rows[direction, at : at + 1, :] = links_ref[
                        part, row, colour, direction : direction + 1, :
                    ]

    pl.semaphore_wait(barrier, NS - 1 + slices - 1 + 7)

    gathers = []
    for step in range(1, NS):
        copy = pltpu.make_async_remote_copy(
            src_ref=gathered.at[0], dst_ref=gathered.at[step],
            send_sem=gather_s.at[step], recv_sem=gather_r.at[step],
            device_id=src_peer(step), device_id_type=MESH,
        )
        copy.start()
        gathers.append(copy)
    link_copies = []
    for direction in range(4):
        copy = pltpu.make_async_remote_copy(
            src_ref=link_rows.at[direction], dst_ref=link_in.at[direction],
            send_sem=link_s.at[direction], recv_sem=link_r.at[direction],
            device_id=(ahead[direction], mine), device_id_type=MESH,
        )
        copy.start()
        link_copies.append(copy)
    for copy in gathers:
        copy.wait()

    for step in range(NS):
        for part in range(2):
            trans[pl.ds(part * NS + step, 16, stride=8), :] = gathered[step, part].astype(F32)

    def table(pair):
        halves = [
            jnp.concatenate([comp_ref[part, 2 * pair], comp_ref[part, 2 * pair + 1]], axis=1)
            for part in range(2)
        ]
        return jnp.concatenate(halves, axis=0)

    summed = jnp.zeros((8, 256), F32)
    for pair in range(6):
        rows = jnp.concatenate(
            [trans[16 * pair : 16 * pair + 8, :], trans[16 * pair + 8 : 16 * pair + 16, :]], axis=1
        )
        summed += dot_nt(rows.astype(BF16), table(pair))
    upper_rows = lax.broadcasted_iota(jnp.int32, (8, 128), 0) < NS
    turned = pltpu.roll(summed[:, 128:256], NS, 0)
    amplitude = summed[:, 0:128] + jnp.where(upper_rows, turned, -turned)

    def exchange(slots, here, count, peer, send_sems, recv_sems):
        copies = []
        for step in range(1, count):
            copy = pltpu.make_async_remote_copy(
                src_ref=slots.at[here], dst_ref=slots.at[here],
                send_sem=send_sems.at[step], recv_sem=recv_sems.at[step],
                device_id=peer(step), device_id_type=MESH,
            )
            copy.start()
            copies.append(copy)
        for copy in copies:
            copy.wait()

    sums_t[pl.ds(time, 1)] = amplitude[None]
    exchange(sums_t, time, slices, time_peer, t_s, t_r)
    sums_y[pl.ds(place, 1)] = jnp.sum(sums_t[...], axis=0, keepdims=True)
    exchange(sums_y, place, 8, place_peer, y_s, y_r)
    amplitude = jnp.sum(sums_y[...], axis=0)

    weights = (amplitude / eig_ref[...]).astype(BF16).astype(F32)
    turned = pltpu.roll(weights, NS, 0)
    weights = jnp.concatenate([weights, jnp.where(upper_rows, -turned, turned)], axis=1).astype(BF16)
    for pair in range(6):
        out = dot_nn(weights, table(pair))
        trans[16 * pair : 16 * pair + 8, :] = out[:, 0:128]
        trans[16 * pair + 8 : 16 * pair + 16, :] = out[:, 128:256]
    for step in range(NS):
        for part in range(2):
            parts[step, part] = trans[pl.ds(part * NS + step, 16, stride=8), :]
    sends = []
    for step in range(1, NS):
        copy = pltpu.make_async_remote_copy(
            src_ref=parts.at[step], dst_ref=incoming.at[step],
            send_sem=parts_s.at[step], recv_sem=parts_r.at[step],
            device_id=src_peer(NS - step), device_id_type=MESH,
        )
        copy.start()
        sends.append(copy)
    for copy in sends:
        copy.wait()
    coarse = [
        (parts[0, part] + incoming[1, part] + incoming[2, part] + incoming[3, part]).astype(BF16)
        for part in range(2)
    ]
    left = jnp.concatenate(
        [
            jnp.concatenate([coarse[0], -coarse[1]], axis=1),
            jnp.concatenate([coarse[1], coarse[0]], axis=1),
        ],
        axis=0,
    )
    for a in range(12):
        guess_out[a] = dot_nn(left, basis_ref[:, a].reshape(2 * NV, VOL))

    def load(a):
        return guess_out[a, 0:16, :], guess_out[a, 16:32, :]

    copies = []
    for direction in (3, 2, 1, 0):
        minus, plus = half_spinors(direction, load)
        for values, level, send, land, peer, send_sems, recv_sems in (
            (minus, 0, fwd_send, fwd_in, behind, fwd_s, fwd_r),
            (plus, EDGE - 1, bwd_send, bwd_in, ahead, bwd_s, bwd_r),
        ):
            low, high = site_selector(direction, level)
            flat = [item.astype(BF16) for pair in values for item in pair]
            packed = dot_nn(jnp.concatenate(flat[:6], axis=0), low)
            packed += dot_nn(jnp.concatenate(flat[6:], axis=0), high)
            send[direction] = packed.astype(BF16)
            copy = pltpu.make_async_remote_copy(
                src_ref=send.at[direction], dst_ref=land.at[direction],
                send_sem=send_sems.at[direction], recv_sem=recv_sems.at[direction],
                device_id=(peer[direction], mine), device_id_type=MESH,
            )
            copy.start()
            copies.append(copy)
    for copy in link_copies:
        copy.wait()
    for copy in copies:
        copy.wait()
    fwd_out[...] = fwd_in[...]
    bwd_out[...] = bwd_in[...]
    rlinks_out[...] = link_in[...]


def dirac_kernel(
    src_ref, guess_ref, links_ref, rlinks_ref, fwd_ref, bwd_ref, out_ref,
    hop, halo_f, halo_b, link_rows,
):
    lane = lax.broadcasted_iota(jnp.int32, (24, VOL), 1)
    for direction in range(4):
        for part in range(2):
            for row in range(3):
                for colour in range(3):
                    at = part * 9 + row * 3 + colour
                    link_rows[direction, at : at + 1, :] = links_ref[
                        part, row, colour, direction : direction + 1, :
                    ]
    for direction in range(4):
        stride = EDGE**direction
        edge = (lane // stride) % EDGE == 0
        link_rows[4 + direction] = jnp.where(
            edge,
            pltpu.roll(rlinks_ref[direction], VOL - 3 * stride, 1),
            pltpu.roll(link_rows[direction], stride, 1),
        )
        for source, level, halo in ((fwd_ref, EDGE - 1, halo_f), (bwd_ref, 0, halo_b)):
            low, high = site_selector(direction, level)
            halo[direction, 0:96] = dot_nt(source[direction], low)
            halo[direction, 96:192] = dot_nt(source[direction], high)

    lane8 = lax.broadcasted_iota(jnp.int32, (8, VOL), 1)

    def group(index, carry):
        base = pl.multiple_of(index * 8, 8)

        def load(a):
            return guess_ref[a, pl.ds(base, 8), :], guess_ref[a, pl.ds(base + 16, 8), :]

        for direction in range(4):
            stride = EDGE**direction
            coord = (lane8 // stride) % EDGE
            minus, plus = half_spinors(direction, load)

            def shifted(values, halo, amount, edge):
                result = []
                for comp in range(6):
                    result.append(
                        tuple(
                            jnp.where(
                                coord == edge,
                                halo[direction, pl.ds(base + comp * 32 + 16 * part, 8), :],
                                pltpu.roll(values[comp][part], amount, 1),
                            )
                            for part in range(2)
                        )
                    )
                return result

            forward = shifted(minus, halo_f, VOL - stride, EDGE - 1)
            backward = shifted(plus, halo_b, stride, 0)

            def link(which, part, row, colour):
                at = part * 9 + row * 3 + colour
                return link_rows[which, at : at + 1, :]

            moved = [None] * 6
            back = [None] * 6
            for row in range(3):
                for spin in range(2):
                    real = imag = 0.0
                    for colour in range(3):
                        link_re = link(direction, 0, row, colour)
                        link_im = link(direction, 1, row, colour)
                        re, im = forward[3 * spin + colour]
                        real = real + (link_re * re - link_im * im)
                        imag = imag + (link_re * im + link_im * re)
                    moved[3 * spin + row] = (real, imag)
                    real = imag = 0.0
                    for colour in range(3):
                        link_re = link(4 + direction, 0, colour, row)
                        link_im = link(4 + direction, 1, colour, row)
                        re, im = backward[3 * spin + colour]
                        real = real + (link_re * re + link_im * im)
                        imag = imag + (link_re * im - link_im * re)
                    back[3 * spin + row] = (real, imag)
            for colour in range(3):
                first = sub(back[colour], moved[colour])
                second = sub(back[3 + colour], moved[3 + colour])
                lowers = spin_e_dagger(direction, first, second)
                totals = [
                    add(back[colour], moved[colour]),
                    add(back[3 + colour], moved[3 + colour]),
                    lowers[0],
                    lowers[1],
                ]
                for spin in range(4):
                    for part in range(2):
                        rows = pl.ds(base + 16 * part, 8)
                        value = totals[spin][part]
                        if direction == 0:
                            hop[3 * spin + colour, rows, :] = value
                        else:
                            hop[3 * spin + colour, rows, :] += value
        return carry

    lax.fori_loop(0, 2, group, 0)

    for a in range(12):
        for part in range(2):
            rows = slice(part * 16, part * 16 + LS)
            value = guess_ref[a, rows, :]
            if a < 6:
                fifth = jnp.concatenate([-FIFTH_MASS * value[LS - 1 : LS], value[0 : LS - 1]], axis=0)
            else:
                fifth = jnp.concatenate([value[1:LS], -FIFTH_MASS * value[0:1]], axis=0)
            applied = (5.0 - WALL_HEIGHT) * value - 0.5 * hop[a, rows, :] - fifth
            for half in range(2):
                at = pl.ds(24 * (part * 12 + a) + half, LS, stride=2)
                out_ref[at, :] = src_ref[at, :] - applied[:, half * 128 : half * 128 + 128]


def body(blocks, source, basis, compressed, eigenvalues, links):
    flat_source = source.reshape(2 * 12 * LS * 2, 128)
    table = jnp.transpose(compressed.reshape(2, 128, LS, NV), (0, 2, 1, 3))
    link_table = jnp.transpose(links, (0, 2, 3, 1, 4))
    eig = eigenvalues.reshape(1, 128)
    vmem = pl.BlockSpec(memory_space=pltpu.VMEM)
    dma = pltpu.SemaphoreType.DMA
    guess, fwd, bwd, rlinks = pl.pallas_call(
        functools.partial(guess_kernel, blocks),
        out_shape=(
            jax.ShapeDtypeStruct((12, 32, VOL), F32),
            jax.ShapeDtypeStruct((4, 96, 128), BF16),
            jax.ShapeDtypeStruct((4, 96, 128), BF16),
            jax.ShapeDtypeStruct((4, 24, VOL), F32),
        ),
        in_specs=[vmem] * 5,
        out_specs=(vmem,) * 4,
        scratch_shapes=[
            pltpu.VMEM((12, 32, VOL), F32),
            pltpu.VMEM((NS, 2, 16, 128), BF16),
            pltpu.VMEM((128, 128), F32),
            pltpu.VMEM((NS, 2, 16, 128), F32),
            pltpu.VMEM((NS, 2, 16, 128), F32),
            pltpu.VMEM((blocks // 8, 8, 128), F32),
            pltpu.VMEM((8, 8, 128), F32),
            pltpu.VMEM((4, 24, VOL), F32),
            pltpu.VMEM((4, 24, VOL), F32),
            pltpu.VMEM((4, 96, 128), BF16),
            pltpu.VMEM((4, 96, 128), BF16),
            pltpu.VMEM((4, 96, 128), BF16),
            pltpu.VMEM((4, 96, 128), BF16),
            dma((NS,)), dma((NS,)), dma((NS,)), dma((NS,)),
            dma((blocks // 8,)), dma((blocks // 8,)), dma((8,)), dma((8,)),
            dma((4,)), dma((4,)), dma((4,)), dma((4,)), dma((4,)), dma((4,)),
        ],
        compiler_params=pltpu.CompilerParams(
            collective_id=0, has_side_effects=True, vmem_limit_bytes=VMEM_LIMIT
        ),
        name="deflated_guess",
    )(flat_source, basis, table, eig, link_table)
    residual = pl.pallas_call(
        dirac_kernel,
        out_shape=jax.ShapeDtypeStruct((576, 128), F32),
        in_specs=[vmem] * 6,
        out_specs=vmem,
        scratch_shapes=[
            pltpu.VMEM((12, 32, VOL), F32),
            pltpu.VMEM((4, 192, VOL), F32),
            pltpu.VMEM((4, 192, VOL), F32),
            pltpu.VMEM((8, 24, VOL), F32),
        ],
        compiler_params=pltpu.CompilerParams(vmem_limit_bytes=VMEM_LIMIT),
        name="dirac",
    )(flat_source, guess, link_table, rlinks, fwd, bwd)
    return residual.reshape(source.shape)


def solution(mesh):
    in_specs = (
        P(None, None, "src", None, "site"),
        P(None, None, None, "site"),
        P(None, "src", "site", None, None),
        P("src"),
        P(None, None, None, None, "site"),
    )
    out_specs = P(None, None, "src", None, "site")
    step = functools.partial(body, mesh.shape["site"])
    return jax.shard_map(step, mesh=mesh, in_specs=in_specs, out_specs=out_specs, check_vma=False)
```

```python
import functools

import jax
import jax.numpy as jnp
from jax import lax
from jax.experimental import pallas as pl
from jax.experimental.pallas import tpu as pltpu
from jax.sharding import PartitionSpec as P

MESH = pl.DeviceIdType.MESH
F32 = jnp.float32
BF16 = jnp.bfloat16

EDGE = 4
LS = 12
NV = 128
VOL = EDGE**4
NS = 4
FIFTH_MASS = 0.4
WALL_HEIGHT = 1.8
VMEM_LIMIT = 64 * 1024 * 1024


def dot_nt(left, right):
    return lax.dot_general(left, right, (((1,), (1,)), ((), ())), preferred_element_type=F32)


def dot_nn(left, right):
    return jnp.dot(left, right, preferred_element_type=F32)


def site_selector(direction, level):
    stride = EDGE**direction
    lane = lax.broadcasted_iota(jnp.int32, (VOL, 128), 0)
    col = lax.broadcasted_iota(jnp.int32, (VOL, 128), 1)
    cell = col & 63
    site = (cell & (stride - 1)) + level * stride + (cell // stride) * (stride * EDGE)
    match = lane == site
    low = jnp.where(match & (col < 64), 1.0, 0.0).astype(BF16)
    high = jnp.where(match & (col >= 64), 1.0, 0.0).astype(BF16)
    return low, high


def times_i(value):
    return (-value[1], value[0])


def neg(value):
    return (-value[0], -value[1])


def add(left, right):
    return (left[0] + right[0], left[1] + right[1])


def sub(left, right):
    return (left[0] - right[0], left[1] - right[1])


def spin_e(direction, first, second):
    if direction == 0:
        return times_i(second), times_i(first)
    if direction == 1:
        return second, neg(first)
    if direction == 2:
        return times_i(first), neg(times_i(second))
    return first, second


def spin_e_dagger(direction, first, second):
    if direction == 0:
        return neg(times_i(second)), neg(times_i(first))
    if direction == 1:
        return neg(second), first
    if direction == 2:
        return neg(times_i(first)), times_i(second)
    return first, second


def half_spinors(direction, load):
    minus = [None] * 6
    plus = [None] * 6
    for colour in range(3):
        lowers = spin_e(direction, load(6 + colour), load(9 + colour))
        for spin in range(2):
            upper = load(3 * spin + colour)
            minus[3 * spin + colour] = sub(upper, lowers[spin])
            plus[3 * spin + colour] = add(upper, lowers[spin])
    return minus, plus


def neighbours(block, blocks):
    ahead = []
    behind = []
    for direction in range(3):
        step = 1 << direction
        other = block + step - 2 * step * ((block // step) % 2)
        ahead.append(other)
        behind.append(other)
    ahead.append((block + 8) % blocks)
    behind.append((block + blocks - 8) % blocks)
    return ahead, behind


def fused_kernel(
    blocks,
    src_hbm, basis_hbm, comp_hbm, eig_hbm, links_hbm,
    out_ref,
    src_ref, basis_ref, comp_ref, eig_ref, links_ref,
    low_src, gathered, trans, parts, incoming, sums_t, sums_y,
    link_rows, link_in, link_back, selectors, guess, total, halo_f, halo_b,
    fwd_send, bwd_send, fwd_in, bwd_in,
    load_s, gather_s, gather_r, parts_s, parts_r, t_s, t_r, y_s, y_r,
    link_s, link_r, fwd_s, fwd_r, bwd_s, bwd_r,
):
    block = lax.axis_index("site")
    mine = lax.axis_index("src")
    slices = blocks // 8
    time = block // 8
    place = block % 8
    ahead, behind = neighbours(block, blocks)

    def src_peer(step):
        return (block, (mine + step) % NS)

    def time_peer(step):
        return (((time + step) % slices) * 8 + place, mine)

    def place_peer(step):
        return (time * 8 + (place + step) % 8, mine)

    loads = []
    for index, (far, near) in enumerate(
        (
            (src_hbm, src_ref), (basis_hbm, basis_ref), (links_hbm, links_ref),
            (comp_hbm, comp_ref), (eig_hbm, eig_ref),
        )
    ):
        copy = pltpu.make_async_copy(far, near, load_s.at[index])
        copy.start()
        loads.append(copy)

    barrier = pltpu.get_barrier_semaphore()
    for count, peer in ((NS, src_peer), (slices, time_peer), (8, place_peer)):
        for step in range(1, count):
            pl.semaphore_signal(barrier, inc=1, device_id=peer(step), device_id_type=MESH)

    loads[0].wait()
    for a in range(12):
        for part in range(2):
            for half in range(2):
                rows = src_ref[pl.ds(24 * (part * 12 + a) + half, LS, stride=2), :]
                low_src[a, part * 16 : part * 16 + LS, half * 128 : half * 128 + 128] = rows
    loads[1].wait()
    product = jnp.zeros((32, 256), F32)
    for a in range(12):
        tile = basis_ref[:, a].reshape(2 * NV, VOL)
        product += dot_nt(low_src[a].astype(BF16), tile)
    gathered[0, 0] = (product[0:16, 0:128] + product[16:32, 128:256]).astype(BF16)
    gathered[0, 1] = (product[16:32, 0:128] - product[0:16, 128:256]).astype(BF16)

    pl.semaphore_wait(barrier, NS - 1 + slices - 1 + 7)

    sent = []

    def send(source, target, send_sem, recv_sem, peer):
        copy = pltpu.make_async_remote_copy(
            src_ref=source, dst_ref=target, send_sem=send_sem, recv_sem=recv_sem,
            device_id=peer, device_id_type=MESH,
        )
        copy.start()
        sent.append(copy)
        return copy

    gathers = [
        send(gathered.at[0], gathered.at[step], gather_s.at[step], gather_r.at[step], src_peer(step))
        for step in range(1, NS)
    ]

    loads[2].wait()
    for direction in range(4):
        for part in range(2):
            for row in range(3):
                for colour in range(3):
                    at = part * 9 + row * 3 + colour
                    link_rows[direction, at : at + 1, :] = (
                        0.5 * links_ref[part, row, colour, direction : direction + 1, :]
                    )
    link_copies = [
        send(
            link_rows.at[direction], link_in.at[direction],
            link_s.at[direction], link_r.at[direction], (ahead[direction], mine),
        )
        for direction in range(4)
    ]
    loads[3].wait()
    loads[4].wait()
    for copy in gathers:
        copy.wait_recv()

    for step in range(NS):
        for part in range(2):
            trans[pl.ds(part * NS + step, 16, stride=8), :] = gathered[step, part].astype(F32)

    def table(pair):
        halves = [
            jnp.concatenate([comp_ref[part, 2 * pair], comp_ref[part, 2 * pair + 1]], axis=1)
            for part in range(2)
        ]
        return jnp.concatenate(halves, axis=0)

    summed = jnp.zeros((8, 256), F32)
    for pair in range(6):
        rows = jnp.concatenate(
            [trans[16 * pair : 16 * pair + 8, :], trans[16 * pair + 8 : 16 * pair + 16, :]], axis=1
        )
        summed += dot_nt(rows.astype(BF16), table(pair))
    upper_rows = lax.broadcasted_iota(jnp.int32, (8, 128), 0) < NS
    turned = pltpu.roll(summed[:, 128:256], NS, 0)
    amplitude = summed[:, 0:128] + jnp.where(upper_rows, turned, -turned)

    def exchange(slots, here, count, peer, send_sems, recv_sems):
        return [
            send(slots.at[here], slots.at[here], send_sems.at[step], recv_sems.at[step], peer(step))
            for step in range(1, count)
        ]

    sums_t[pl.ds(time, 1)] = amplitude[None]
    copies = exchange(sums_t, time, slices, time_peer, t_s, t_r)
    for direction in range(4):
        for index, level in enumerate((0, EDGE - 1)):
            low, high = site_selector(direction, level)
            selectors[direction, index, 0] = low
            selectors[direction, index, 1] = high
    for copy in copies:
        copy.wait_recv()
    sums_y[pl.ds(place, 1)] = jnp.sum(sums_t[...], axis=0, keepdims=True)
    copies = exchange(sums_y, place, 8, place_peer, y_s, y_r)
    for copy in link_copies:
        copy.wait_recv()
    lane = lax.broadcasted_iota(jnp.int32, (24, VOL), 1)
    for direction in range(4):
        stride = EDGE**direction
        link_back[direction] = jnp.where(
            (lane // stride) % EDGE == 0,
            pltpu.roll(link_in[direction], VOL - 3 * stride, 1),
            pltpu.roll(link_rows[direction], stride, 1),
        )
    for copy in copies:
        copy.wait_recv()
    amplitude = jnp.sum(sums_y[...], axis=0)

    weights = (amplitude / eig_ref[...]).astype(BF16).astype(F32)
    turned = pltpu.roll(weights, NS, 0)
    weights = jnp.concatenate([weights, jnp.where(upper_rows, -turned, turned)], axis=1).astype(BF16)
    for pair in range(6):
        out = dot_nn(weights, table(pair))
        trans[16 * pair : 16 * pair + 8, :] = out[:, 0:128]
        trans[16 * pair + 8 : 16 * pair + 16, :] = out[:, 128:256]
    for step in range(NS):
        for part in range(2):
            parts[step, part] = trans[pl.ds(part * NS + step, 16, stride=8), :]
    copies = [
        send(parts.at[step], incoming.at[step], parts_s.at[step], parts_r.at[step], src_peer(NS - step))
        for step in range(1, NS)
    ]
    for copy in copies:
        copy.wait_recv()
    coarse = [
        (parts[0, part] + incoming[1, part] + incoming[2, part] + incoming[3, part]).astype(BF16)
        for part in range(2)
    ]
    left = jnp.concatenate(
        [
            jnp.concatenate([coarse[0], -coarse[1]], axis=1),
            jnp.concatenate([coarse[1], coarse[0]], axis=1),
        ],
        axis=0,
    )
    for a in range(12):
        guess[a] = dot_nn(left, basis_ref[:, a].reshape(2 * NV, VOL))

    def load(a):
        return guess[a, 0:16, :], guess[a, 16:32, :]

    order = (2, 3, 1, 0)
    faces = {}
    for direction in order:
        minus, plus = half_spinors(direction, load)
        faces[direction] = []
        for values, index, out, land, peer, send_sems, recv_sems in (
            (minus, 0, fwd_send, fwd_in, behind, fwd_s, fwd_r),
            (plus, 1, bwd_send, bwd_in, ahead, bwd_s, bwd_r),
        ):
            flat = [item.astype(BF16) for pair in values for item in pair]
            packed = dot_nn(jnp.concatenate(flat[:6], axis=0), selectors[direction, index, 0])
            packed += dot_nn(jnp.concatenate(flat[6:], axis=0), selectors[direction, index, 1])
            out[direction] = packed.astype(BF16)
            faces[direction].append(
                send(
                    out.at[direction], land.at[direction],
                    send_sems.at[direction], recv_sems.at[direction], (peer[direction], mine),
                )
            )

    for a in range(12):
        for part in range(2):
            rows = slice(part * 16, part * 16 + LS)
            value = guess[a, rows, :]
            if a < 6:
                fifth = jnp.concatenate([-FIFTH_MASS * value[LS - 1 : LS], value[0 : LS - 1]], axis=0)
            else:
                fifth = jnp.concatenate([value[1:LS], -FIFTH_MASS * value[0:1]], axis=0)
            total[a, rows, :] = low_src[a, rows, :] - (5.0 - WALL_HEIGHT) * value + fifth

    lane8 = lax.broadcasted_iota(jnp.int32, (8, VOL), 1)
    for direction in reversed(order):
        for copy, source, index, halo in zip(
            faces[direction], (fwd_in, bwd_in), (1, 0), (halo_f, halo_b), strict=True
        ):
            copy.wait_recv()
            halo[0:96] = dot_nt(source[direction], selectors[direction, index, 0])
            halo[96:192] = dot_nt(source[direction], selectors[direction, index, 1])

        def group(which, carry, direction=direction):
            base = pl.multiple_of(which * 8, 8)
            stride = EDGE**direction
            coord = (lane8 // stride) % EDGE

            def rows_of(a):
                return guess[a, pl.ds(base, 8), :], guess[a, pl.ds(base + 16, 8), :]

            minus, plus = half_spinors(direction, rows_of)

            def shifted(values, halo, amount, edge):
                return [
                    tuple(
                        jnp.where(
                            coord == edge,
                            halo[pl.ds(base + comp * 32 + 16 * part, 8), :],
                            pltpu.roll(values[comp][part], amount, 1),
                        )
                        for part in range(2)
                    )
                    for comp in range(6)
                ]

            forward = shifted(minus, halo_f, VOL - stride, EDGE - 1)
            backward = shifted(plus, halo_b, stride, 0)

            def link(rows, part, row, colour):
                at = part * 9 + row * 3 + colour
                return rows[direction, at : at + 1, :]

            moved = [None] * 6
            back = [None] * 6
            for row in range(3):
                for spin in range(2):
                    real = imag = 0.0
                    for colour in range(3):
                        link_re = link(link_rows, 0, row, colour)
                        link_im = link(link_rows, 1, row, colour)
                        re, im = forward[3 * spin + colour]
                        real = real + (link_re * re - link_im * im)
                        imag = imag + (link_re * im + link_im * re)
                    moved[3 * spin + row] = (real, imag)
                    real = imag = 0.0
                    for colour in range(3):
                        link_re = link(link_back, 0, colour, row)
                        link_im = link(link_back, 1, colour, row)
                        re, im = backward[3 * spin + colour]
                        real = real + (link_re * re + link_im * im)
                        imag = imag + (link_re * im - link_im * re)
                    back[3 * spin + row] = (real, imag)
            for colour in range(3):
                first = sub(back[colour], moved[colour])
                second = sub(back[3 + colour], moved[3 + colour])
                lowers = spin_e_dagger(direction, first, second)
                totals = [
                    add(back[colour], moved[colour]),
                    add(back[3 + colour], moved[3 + colour]),
                    lowers[0],
                    lowers[1],
                ]
                for spin in range(4):
                    for part in range(2):
                        rows = pl.ds(base + 16 * part, 8)
                        total[3 * spin + colour, rows, :] += totals[spin][part]
            return carry

        lax.fori_loop(0, 2, group, 0)

    for a in range(12):
        for part in range(2):
            for half in range(2):
                out_ref[pl.ds(24 * (part * 12 + a) + half, LS, stride=2), :] = total[
                    a, part * 16 : part * 16 + LS, half * 128 : half * 128 + 128
                ]
    for copy in sent:
        copy.wait_send()


def body(blocks, source, basis, compressed, eigenvalues, links):
    flat_source = source.reshape(2 * 12 * LS * 2, 128)
    table = jnp.transpose(compressed.reshape(2, 128, LS, NV), (0, 2, 1, 3))
    link_table = jnp.transpose(links, (0, 2, 3, 1, 4))
    eig = eigenvalues.reshape(1, 128)
    dma = pltpu.SemaphoreType.DMA
    residual = pl.pallas_call(
        functools.partial(fused_kernel, blocks),
        out_shape=jax.ShapeDtypeStruct((576, 128), F32),
        in_specs=[pl.BlockSpec(memory_space=pltpu.HBM)] * 5,
        out_specs=pl.BlockSpec(memory_space=pltpu.VMEM),
        scratch_shapes=[
            pltpu.VMEM((576, 128), F32),
            pltpu.VMEM((2, 12, NV, VOL), BF16),
            pltpu.VMEM((2, LS, 128, NV), BF16),
            pltpu.VMEM((1, 128), F32),
            pltpu.VMEM((2, 3, 3, 4, VOL), F32),
            pltpu.VMEM((12, 32, VOL), F32),
            pltpu.VMEM((NS, 2, 16, 128), BF16),
            pltpu.VMEM((128, 128), F32),
            pltpu.VMEM((NS, 2, 16, 128), F32),
            pltpu.VMEM((NS, 2, 16, 128), F32),
            pltpu.VMEM((blocks // 8, 8, 128), F32),
            pltpu.VMEM((8, 8, 128), F32),
            pltpu.VMEM((4, 24, VOL), F32),
            pltpu.VMEM((4, 24, VOL), F32),
            pltpu.VMEM((4, 24, VOL), F32),
            pltpu.VMEM((4, 2, 2, VOL, 128), BF16),
            pltpu.VMEM((12, 32, VOL), F32),
            pltpu.VMEM((12, 32, VOL), F32),
            pltpu.VMEM((192, VOL), F32),
            pltpu.VMEM((192, VOL), F32),
            pltpu.VMEM((4, 96, 128), BF16),
            pltpu.VMEM((4, 96, 128), BF16),
            pltpu.VMEM((4, 96, 128), BF16),
            pltpu.VMEM((4, 96, 128), BF16),
            dma((5,)),
            dma((NS,)), dma((NS,)), dma((NS,)), dma((NS,)),
            dma((blocks // 8,)), dma((blocks // 8,)), dma((8,)), dma((8,)),
            dma((4,)), dma((4,)), dma((4,)), dma((4,)), dma((4,)), dma((4,)),
        ],
        compiler_params=pltpu.CompilerParams(
            collective_id=0, has_side_effects=True, vmem_limit_bytes=VMEM_LIMIT
        ),
        name="deflated_residual",
    )(flat_source, basis, table, eig, link_table)
    return residual.reshape(source.shape)


def solution(mesh):
    in_specs = (
        P(None, None, "src", None, "site"),
        P(None, None, None, "site"),
        P(None, "src", "site", None, None),
        P("src"),
        P(None, None, None, None, "site"),
    )
    out_specs = P(None, None, "src", None, "site")
    step = functools.partial(body, mesh.shape["site"])
    return jax.shard_map(step, mesh=mesh, in_specs=in_specs, out_specs=out_specs, check_vma=False)
```
